32 devices in a mesh: seq: 16 (over z, y, x), tp: 2 (over core).
Axes of the slice: x: 2, y: 2, z: 4, core: 2. Of those that a mesh axis runs over, the one named last changes fastest.
Arguments:
- tokens: bfloat16 [2048, 2048], P('seq'), may hold values from -6 to 6
- cotangent: bfloat16 [2048, 2048], P('seq'), may hold values from -6 to 6
- block_order: int32 [32], replicated, may hold values from 0 to 31, each once
- sequence_ids: int32 [2048], replicated, may hold values from 0 to 1, never falling along the last dimension, each value on 1 to 1536 neighbouring positions
- attn_gain: float32 [2048], P('seq'), may hold values from 0.5 to 1.5
- w_query: float32 [2048, 2048], P('seq', 'tp'), may hold values from -0.125 to 0.125
- w_key: float32 [2048, 2048], P('seq', 'tp'), may hold values from -0.125 to 0.125
- w_value: float32 [2048, 2048], P('seq', 'tp'), may hold values from -0.125 to 0.125
- w_out: float32 [2048, 2048], P('tp', 'seq'), may hold values from -2 to 2
- mlp_gain: float32 [2048], P('seq'), may hold values from 0.5 to 1.5
- w_gate: float32 [2048, 8192], P('seq', 'tp'), may hold values from -0.125 to 0.125
- w_up: float32 [2048, 8192], P('seq', 'tp'), may hold values from -0.125 to 0.125
- w_down: float32 [8192, 2048], P('tp', 'seq'), may hold values from -0.0625 to 0.0625
Outputs:
- output: bfloat16 [2048, 2048], P('seq')
- grad_tokens: float32 [2048, 2048], P('seq')
- grad_attn_gain: float32 [2048], P('seq')
- grad_query: float32 [2048, 2048], P('seq', 'tp')
- grad_key: float32 [2048, 2048], P('seq', 'tp')
- grad_value: float32 [2048, 2048], P('seq', 'tp')
- grad_out: float32 [2048, 2048], P('tp', 'seq')
- grad_mlp_gain: float32 [2048], P('seq')
- grad_gate: float32 [2048, 8192], P('seq', 'tp')
- grad_up: float32 [2048, 8192], P('seq', 'tp')
- grad_down: float32 [8192, 2048], P('tp', 'seq')
The draws below stay inside these ranges and needn't reach their ends.
Inputs may be any that keep to these rules, and one draw needn't show every extreme that they name: `block_order`: each block number appears once. `sequence_ids`: never falls along the positions; the first sequence has from 512 to 1536 tokens and the second the rest.
All inputs are finite; a program needn't handle non-finite values.
Results may differ from the reference program's by a relative error of at most 0.015.
Values may be sent and summed in bfloat16 or wider, within the bound.
A program may use at most 256 MiB of HBM per device.

```python
import math
import jax
import jax.numpy as jnp
import numpy as np
from jax import lax

D = 2048
HEADS = 16
HD = 128
FF = 8192
TOK_DEV = 128
TOKENS = 2048
SEQ_LEN = 1024
GROUPS = 32


def strengthened(values, own_key, source, target, parts, factor):
    owner, partner = [(jnp.arange(values.shape[position]) // (values.shape[position] // parts)).reshape([-1 if axis == position else 1 for axis in range(values.ndim)]) for position in (source, target)]
    chosen = jax.random.permutation(own_key, parts)[partner]
    strong = (owner == chosen) | (owner == (partner + parts // 2) % parts)
    return jnp.where(strong, factor * values, values)


def shard_levels(own_key, extent, cuts, low, high):
    def one(axis_at, blocks):
        heights = jax.random.uniform(jax.random.fold_in(jax.random.fold_in(own_key, 6), axis_at), (blocks,), jnp.float32, low / len(cuts), high / len(cuts))
        return jnp.repeat(jnp.exp(heights), extent[axis_at] // blocks).reshape((-1,) + (1,) * (len(extent) - axis_at - 1))

    factor_of = one(*cuts[0])
    for cut in cuts[1:]:
        factor_of = factor_of * one(*cut)
    return factor_of


def length_profile(number_of, total, most, slope):
    weights = [(1 << 20) // math.isqrt(rank ** slope) + 1 for rank in range(2, number_of + 1)]
    spare, given = total - most - (number_of - 1), [1] * (number_of - 1)
    while spare > 0:
        movable = [i for i in range(number_of - 1) if given[i] < most]
        whole, budget = sum([weights[i] for i in movable]), spare
        for i in movable:
            addition = min(most - given[i], max(1, budget * weights[i] // whole), spare)
            given[i] = given[i] + addition
            spare = spare - addition
    return np.array([most] + given)


def ragged(stream_key, count, total, limit, skew):
    if count == 2:
        one = jax.random.randint(stream_key, (), max(1, total - limit), min(limit, total - 1) + 1)
        return jnp.stack([one, total - one])
    lengths = jnp.asarray(length_profile(count, total, limit, skew), jnp.int32)
    pairs = (count - 1) // 2
    giver, sink = lengths[1:1 + 2 * pairs:2], lengths[2:2 + 2 * pairs:2]
    slack = jnp.minimum(giver - 1, limit - sink)
    moved = jax.random.randint(jax.random.fold_in(stream_key, 1), (pairs,), 0, 1 << 20) % (slack + 1)
    lengths = lengths.at[1:1 + 2 * pairs:2].set(giver - moved).at[2:2 + 2 * pairs:2].set(sink + moved)
    return lengths[jax.random.permutation(jax.random.fold_in(stream_key, 2), count)]


def scatter_about(stream_key, shape, scale, limit, split=(), kind=jnp.bfloat16):
    loudness = shard_levels(stream_key, shape, split, -0.22, 0.18) if split else 1.0
    values = jax.random.normal(stream_key, shape, jnp.float32) * scale * loudness
    return jnp.minimum(jnp.maximum(values, -limit), limit).astype(kind)


def bell_draw_with(stream_key, extent, deviation, bound, shards, heavy, kind=jnp.bfloat16):
    drawn = deviation * jax.random.normal(stream_key, extent, jnp.float32)
    if shards:
        drawn = drawn * shard_levels(stream_key, extent, shards, -0.22, 0.18)
    return jnp.clip(strengthened(drawn, jax.random.fold_in(stream_key, 3), *heavy), -bound, bound).astype(kind)


def setup_inputs(seed: int = 0) -> dict:
    arg_keys = jax.random.split(jax.random.key(seed), 14)
    return {
        "tokens": bell_draw_with(arg_keys[0], (TOKENS, D), 1.0, 6.0, ((0, 16),), (0, 1, 16, 2.0)),
        "cotangent": bell_draw_with(arg_keys[1], (TOKENS, D), 1.0, 6.0, ((0, 16),), (0, 1, 16, 2.0)),
        "block_order": jax.random.permutation(arg_keys[2], GROUPS).astype(jnp.int32),
        "sequence_ids": jnp.searchsorted(jnp.cumsum(ragged(arg_keys[3], 2, TOKENS, 3 * TOKENS // 4, 0)), jnp.arange(TOKENS), side="right").astype(jnp.int32),
        "attn_gain": jnp.clip(1.0 + 0.1 * jax.random.normal(arg_keys[4], (D,), jnp.float32), 0.5, 1.5),
        "w_query": scatter_about(arg_keys[5], (D, HEADS * HD), D ** -0.5, 0.125, ((0, 16), (1, 2)), jnp.float32),
        "w_key": scatter_about(arg_keys[6], (D, HEADS * HD), D ** -0.5, 0.125, ((0, 16), (1, 2)), jnp.float32),
        "w_value": scatter_about(arg_keys[7], (D, HEADS * HD), D ** -0.5, 0.125, ((0, 16), (1, 2)), jnp.float32),
        "w_out": scatter_about(arg_keys[8], (HEADS * HD, D), (max(1, HEADS * HD * 4 // SEQ_LEN)) ** -0.5, 2.0, ((0, 2), (1, 16)), jnp.float32),
        "mlp_gain": jnp.clip(1.0 + 0.1 * jax.random.normal(arg_keys[9], (D,), jnp.float32), 0.5, 1.5),
        "w_gate": scatter_about(arg_keys[10], (D, FF), D ** -0.5, 0.125, ((0, 16), (1, 2)), jnp.float32),
        "w_up": scatter_about(arg_keys[11], (D, FF), D ** -0.5, 0.125, ((0, 16), (1, 2)), jnp.float32),
        "w_down": scatter_about(arg_keys[12], (FF, D), FF ** -0.5, 0.0625, ((0, 2), (1, 16)), jnp.float32),
    }


EPS = 1e-05
ROPE_BASE = 10000.0

@jax.custom_vjp
def low(v):
    return lax.optimization_barrier(v.astype(jnp.bfloat16)).astype(jnp.float32)

@jax.custom_vjp
def low_back(v):
    return v

def low_keep(v):
    return (low(v), None)

def low_pass(kept, grad):
    return (grad,)

def back_keep(v):
    return (v, None)

def back_low(kept, grad):
    return (low(grad),)
low.defvjp(low_keep, low_pass)
low_back.defvjp(back_keep, back_low)

def matmul(left, right):
    return jnp.dot(left, right, precision=lax.Precision.HIGHEST, preferred_element_type=jnp.float32)

def rms_normed(values):
    return values * lax.rsqrt(lax.optimization_barrier(jnp.mean(values * values, axis=-1, keepdims=True)) + EPS)

def rope_tables(positions, head_dim):
    half_dim = head_dim // 2
    freqs = ROPE_BASE ** (-(jnp.arange(half_dim, dtype=jnp.float32) * 2.0 / head_dim))
    angles = positions.astype(jnp.float32)[:, None] * freqs[None, :]
    return (jnp.cos(angles), jnp.sin(angles))

def rotate(field_in, cosine, sine):
    half_dim = field_in.shape[-1] // 2
    first_half = field_in[..., :half_dim]
    second_half = field_in[..., half_dim:]
    cos_part = cosine[:, None, :]
    sin_part = sine[:, None, :]
    return jnp.concatenate([first_half * cos_part - second_half * sin_part, second_half * cos_part + first_half * sin_part], axis=-1)

def attention(queries, keys, values, places, segments, score_bias):
    block_rows = min(512, queries.shape[0])
    blocks = queries.shape[0] // block_rows
    heads_all = queries.shape[1]
    score_scale = 1.0 / math.sqrt(HD)

    def one_block(pieces):
        query_blk, query_pos, query_seg = pieces
        scores = jnp.einsum('qhd,khd->hqk', query_blk, keys, precision=lax.Precision.HIGHEST, preferred_element_type=jnp.float32) * score_scale + score_bias
        scores = low_back(scores)
        allowed = (places[None, :] <= query_pos[:, None]) & (segments[None, :] == query_seg[:, None])
        weights = low(jnp.where(allowed[None], jax.nn.sigmoid(scores), 0.0))
        return jnp.einsum('hqk,khd->qhd', weights, values, precision=lax.Precision.HIGHEST, preferred_element_type=jnp.float32)
    outputs = lax.map(jax.checkpoint(one_block), (queries.reshape(blocks, block_rows, heads_all, HD), places.reshape(blocks, block_rows), segments.reshape(blocks, block_rows)))
    return outputs.reshape(queries.shape[0], heads_all * HD)

def reference(tokens, cotangent, block_order, sequence_ids, attn_gain, w_query, w_key, w_value, w_out, mlp_gain, w_gate, w_up, w_down):
    group_rows = TOK_DEV // 2
    stored = jnp.arange(TOKENS, dtype=jnp.int32)
    positions = (block_order[stored // group_rows] * group_rows + stored % group_rows).astype(jnp.int32)
    inverse = jnp.zeros((TOKENS,), jnp.int32).at[positions].set(stored)
    ordered = tokens.astype(jnp.float32)[inverse]
    ordered_cot = cotangent.astype(jnp.float32)[inverse]
    places = jnp.arange(TOKENS, dtype=jnp.int32)
    cosine, sine = rope_tables(places, HD)
    score_bias = -math.log(SEQ_LEN)

    def forward(source, gain_one, query_weight, key_weight, value_weight, out_weight, gain_two, gate_weight, up_weight, down_weight):
        normed_attn = rms_normed(source)
        hidden_attn = low(normed_attn * low(gain_one))
        heads_all = query_weight.shape[1] // HD
        query_lin = low_back(matmul(hidden_attn, low(query_weight))).reshape(TOKENS, heads_all, HD)
        key_lin = low_back(matmul(hidden_attn, low(key_weight))).reshape(TOKENS, heads_all, HD)
        queries = low(rotate(query_lin, cosine, sine))
        keys = low(rotate(key_lin, cosine, sine))
        values = low(low_back(matmul(hidden_attn, low(value_weight)))).reshape(TOKENS, heads_all, HD)
        attended = low(low_back(attention(queries, keys, values, places, sequence_ids, score_bias)))
        residual = source + low_back(matmul(attended, low(out_weight)))
        normed_mlp = rms_normed(residual)
        hidden_mlp = low(normed_mlp * low(gain_two))
        gate = low_back(matmul(hidden_mlp, low(gate_weight)))
        up_proj = low_back(matmul(hidden_mlp, low(up_weight)))
        activated = low(jax.nn.silu(gate) * up_proj)
        return residual + matmul(activated, low(down_weight))
    result, pullback = jax.vjp(forward, ordered, attn_gain.astype(jnp.float32), w_query.astype(jnp.float32), w_key.astype(jnp.float32), w_value.astype(jnp.float32), w_out.astype(jnp.float32), mlp_gain.astype(jnp.float32), w_gate.astype(jnp.float32), w_up.astype(jnp.float32), w_down.astype(jnp.float32))
    grads = pullback(ordered_cot)
    output = result[positions].astype(jnp.bfloat16)
    grad_tokens = grads[0][positions]
    return (output, grad_tokens, grads[1], grads[2], grads[3], grads[4], grads[5], grads[6], grads[7], grads[8], grads[9])
```

```python
import functools
import math

import jax
import jax.numpy as jnp
from jax import lax
from jax.experimental import pallas as pl
from jax.experimental.pallas import tpu as pltpu
from jax.sharding import PartitionSpec as P

HD = 128


EPS = 1e-05
ROPE_BASE = 10000.0


def from_behind(value, axis, by):
    length = lax.axis_size(axis)
    return lax.ppermute(value, axis, [(i, (i + by) % length) for i in range(length)])


def group_positions(block_order, start, count, group_rows):
    row_ids = start + jnp.arange(count, dtype=jnp.int32)
    which = row_ids // group_rows
    slots = jnp.arange(block_order.shape[0], dtype=jnp.int32)
    onehot = (which[:, None] == slots[None, :]).astype(jnp.int32)
    first_pos = jnp.sum(onehot * block_order[None, :], axis=1)
    return first_pos * group_rows + row_ids % group_rows


def visible(query_pos, key_pos, boundary):
    query_seg = query_pos >= boundary
    key_seg = key_pos >= boundary
    return (key_pos[None, :] <= query_pos[:, None]) & (key_seg[None, :] == query_seg[:, None])


def normalize(values):
    inverse = lax.rsqrt(jnp.mean(values * values, axis=-1, keepdims=True) + EPS)
    return (values * inverse, inverse)


def norm_back(grad_normed, normed, inverse):
    return inverse * (grad_normed - normed * jnp.mean(grad_normed * normed, axis=-1, keepdims=True))


def rope_tables(positions, head_dim):
    half_dim = head_dim // 2
    freqs = ROPE_BASE ** (-(jnp.arange(half_dim, dtype=jnp.float32) * 2.0 / head_dim))
    angles = positions.astype(jnp.float32)[:, None] * freqs[None, :]
    return (jnp.cos(angles), jnp.sin(angles))


def rotate(field_in, cosine, sine):
    half_dim = field_in.shape[-1] // 2
    first_half = field_in[..., :half_dim]
    second_half = field_in[..., half_dim:]
    cos_part = cosine[:, None, :]
    sin_part = sine[:, None, :]
    return jnp.concatenate(
        [
            first_half * cos_part - second_half * sin_part,
            second_half * cos_part + first_half * sin_part,
        ],
        axis=-1,
    )


def unrotate(field_in, cosine, sine):
    half_dim = field_in.shape[-1] // 2
    first_half = field_in[..., :half_dim]
    second_half = field_in[..., half_dim:]
    cos_part = cosine[:, None, :]
    sin_part = sine[:, None, :]
    return jnp.concatenate(
        [
            first_half * cos_part + second_half * sin_part,
            second_half * cos_part - first_half * sin_part,
        ],
        axis=-1,
    )


def pair_terms(
    query_blk,
    gradout_blk,
    query_pos,
    key_blk,
    value_blk,
    key_pos,
    boundary,
    score_scale,
    score_bias,
):
    allowed = visible(query_pos, key_pos, boundary)

    def pair_compute(unused):
        scores = (
            jnp.einsum("qhd,khd->hqk", query_blk, key_blk, preferred_element_type=jnp.float32)
            * score_scale
            + score_bias
        )
        sigmas = jax.nn.sigmoid(scores)
        weights = jnp.where(allowed[None], sigmas, 0.0).astype(jnp.bfloat16)
        grad_vals = jnp.einsum(
            "hqk,qhd->khd", weights, gradout_blk, preferred_element_type=jnp.float32
        )
        grad_weights = jnp.einsum(
            "qhd,khd->hqk", gradout_blk, value_blk, preferred_element_type=jnp.float32
        )
        grad_scores = jnp.where(allowed[None], grad_weights * sigmas * (1.0 - sigmas), 0.0).astype(
            jnp.bfloat16
        )
        grad_qs = (
            jnp.einsum("hqk,khd->qhd", grad_scores, key_blk, preferred_element_type=jnp.float32)
            * score_scale
        )
        grad_ks = (
            jnp.einsum("hqk,qhd->khd", grad_scores, query_blk, preferred_element_type=jnp.float32)
            * score_scale
        )
        return (grad_qs, grad_ks, grad_vals)

    def nothing(unused):
        empty_q = jnp.zeros(query_blk.shape, jnp.float32)
        empty_k = jnp.zeros(key_blk.shape, jnp.float32)
        return (empty_q, empty_k, empty_k)

    return lax.cond(jnp.any(allowed), pair_compute, nothing, 0)


def per_device_gathered(
    tokens,
    cotangent,
    block_order,
    sequence_ids,
    attn_gain,
    w_query,
    w_key,
    w_value,
    w_out,
    mlp_gain,
    w_gate,
    w_up,
    w_down,
):
    tok_rows = tokens.shape[0]
    group_rows = tok_rows // 2
    devices = lax.axis_size("seq")
    score_bias = -math.log(tok_rows * devices // 2)
    score_scale = 1.0 / math.sqrt(HD)
    my_index = lax.axis_index("seq")
    boundary = jnp.sum((sequence_ids == 0).astype(jnp.int32))
    my_pos = group_positions(block_order, my_index * tok_rows, tok_rows, group_rows)
    attn_parts = (
        lax.all_gather(w_query.astype(jnp.bfloat16), "seq", axis=0, tiled=True),
        lax.all_gather(w_key.astype(jnp.bfloat16), "seq", axis=0, tiled=True),
        lax.all_gather(w_value.astype(jnp.bfloat16), "seq", axis=0, tiled=True),
        lax.all_gather(w_out.astype(jnp.bfloat16), "seq", axis=1, tiled=True),
        lax.all_gather(attn_gain.astype(jnp.bfloat16), "seq", axis=0, tiled=True),
    )
    query_full, key_full, value_full, out_full = (
        attn_parts[0],
        attn_parts[1],
        attn_parts[2],
        attn_parts[3],
    )
    gain_attn = attn_parts[4].astype(jnp.float32)
    heads_local = query_full.shape[1] // HD
    source = tokens.astype(jnp.float32)
    normed_attn, inverse_attn = normalize(source)
    hidden_attn = (normed_attn * gain_attn).astype(jnp.bfloat16)
    cosine, sine = rope_tables(my_pos, HD)

    def project(weight_full):
        return jnp.dot(hidden_attn, weight_full, preferred_element_type=jnp.float32).reshape(
            tok_rows, heads_local, HD
        )

    queries = rotate(project(query_full), cosine, sine).astype(jnp.bfloat16)
    keys = rotate(project(key_full), cosine, sine).astype(jnp.bfloat16)
    values = project(value_full).astype(jnp.bfloat16)
    key_all = lax.all_gather(keys, "seq", axis=0, tiled=True)
    value_all = lax.all_gather(values, "seq", axis=0, tiled=True)
    piece_rows = key_all.shape[0]
    block_rows = math.gcd(piece_rows, 512)

    def add_block(block_index, partial_value):
        offset = block_index * block_rows
        key_blk = lax.dynamic_slice_in_dim(key_all, offset, block_rows, 0)
        value_blk = lax.dynamic_slice_in_dim(value_all, offset, block_rows, 0)
        key_pos = group_positions(block_order, offset, block_rows, group_rows)
        allowed = visible(my_pos, key_pos, boundary)

        def add_compute(current):
            scores = (
                jnp.einsum("qhd,khd->hqk", queries, key_blk, preferred_element_type=jnp.float32)
                * score_scale
                + score_bias
            )
            weights = jnp.where(allowed[None], jax.nn.sigmoid(scores), 0.0).astype(jnp.bfloat16)
            return current + jnp.einsum(
                "hqk,khd->qhd", weights, value_blk, preferred_element_type=jnp.float32
            )

        def unchanged(current):
            return current

        return lax.cond(jnp.any(allowed), add_compute, unchanged, partial_value)

    attended = lax.fori_loop(
        0, piece_rows // block_rows, add_block, jnp.zeros((tok_rows, heads_local, HD), jnp.float32)
    )
    attended_low = attended.reshape(tok_rows, heads_local * HD).astype(jnp.bfloat16)
    attn_part = jnp.dot(attended_low, out_full, preferred_element_type=jnp.float32)
    residual = source + lax.psum(attn_part, "tp")
    mlp_parts = (
        lax.all_gather(w_gate.astype(jnp.bfloat16), "seq", axis=0, tiled=True),
        lax.all_gather(w_up.astype(jnp.bfloat16), "seq", axis=0, tiled=True),
        lax.all_gather(w_down.astype(jnp.bfloat16), "seq", axis=1, tiled=True),
        lax.all_gather(mlp_gain.astype(jnp.bfloat16), "seq", axis=0, tiled=True),
    )
    gate_full, up_full, down_full = (mlp_parts[0], mlp_parts[1], mlp_parts[2])
    gain_mlp = mlp_parts[3].astype(jnp.float32)
    normed_mlp, inverse_mlp = normalize(residual)
    hidden_mlp = (normed_mlp * gain_mlp).astype(jnp.bfloat16)
    gate = jnp.dot(hidden_mlp, gate_full, preferred_element_type=jnp.float32)
    up_proj = jnp.dot(hidden_mlp, up_full, preferred_element_type=jnp.float32)
    gate_sigma = jax.nn.sigmoid(gate)
    gate_silu = gate * gate_sigma
    activated = (gate_silu * up_proj).astype(jnp.bfloat16)
    mlp_part = jnp.dot(activated, down_full, preferred_element_type=jnp.float32)
    output = (residual + lax.psum(mlp_part, "tp")).astype(jnp.bfloat16)
    grad_w_down = jnp.einsum("tf,td->fd", activated, cotangent, preferred_element_type=jnp.float32)
    grad_act = jnp.einsum("td,fd->tf", cotangent, down_full, preferred_element_type=jnp.float32)
    grad_gate_act = (grad_act * up_proj * gate_sigma * (1.0 + gate * (1.0 - gate_sigma))).astype(
        jnp.bfloat16
    )
    grad_up_act = (grad_act * gate_silu).astype(jnp.bfloat16)
    grad_w_gate = jnp.einsum(
        "td,tf->df", hidden_mlp, grad_gate_act, preferred_element_type=jnp.float32
    )
    grad_w_up = jnp.einsum("td,tf->df", hidden_mlp, grad_up_act, preferred_element_type=jnp.float32)
    hidden_grad_part = jnp.einsum(
        "tf,df->td", grad_gate_act, gate_full, preferred_element_type=jnp.float32
    ) + jnp.einsum("tf,df->td", grad_up_act, up_full, preferred_element_type=jnp.float32)
    grad_hidden_mlp = lax.psum(hidden_grad_part, "tp")
    grad_gain_mlp = jnp.sum(grad_hidden_mlp * normed_mlp, axis=0)
    grad_resid = norm_back(grad_hidden_mlp * gain_mlp, normed_mlp, inverse_mlp) + cotangent.astype(
        jnp.float32
    )
    mlp_shards = (
        lax.psum_scatter(grad_w_gate, "seq", scatter_dimension=0, tiled=True),
        lax.psum_scatter(grad_w_up, "seq", scatter_dimension=0, tiled=True),
        lax.psum_scatter(grad_w_down, "seq", scatter_dimension=1, tiled=True),
        lax.psum_scatter(grad_gain_mlp, "seq", scatter_dimension=0, tiled=True),
    )
    resid_low = grad_resid.astype(jnp.bfloat16)
    grad_w_out = jnp.einsum(
        "tc,td->cd", attended_low, resid_low, preferred_element_type=jnp.float32
    )
    grad_attended = (
        jnp.einsum("td,cd->tc", resid_low, out_full, preferred_element_type=jnp.float32)
        .astype(jnp.bfloat16)
        .reshape(tok_rows, heads_local, HD)
    )
    zero_rows = jnp.zeros((tok_rows, heads_local, HD), jnp.float32)

    def key_turn(turn, carry):
        moving, moving_grads, grad_qsum = carry
        source_index = (my_index + turn) % devices
        key_pos = group_positions(block_order, source_index * tok_rows, tok_rows, group_rows)
        terms = pair_terms(
            queries,
            grad_attended,
            my_pos,
            moving[0],
            moving[1],
            key_pos,
            boundary,
            score_scale,
            score_bias,
        )
        moving_grads = moving_grads + jnp.stack([terms[1], terms[2]])
        moving = from_behind(moving, "seq", -1)
        moving_grads = from_behind(moving_grads, "seq", -1)
        return (moving, moving_grads, grad_qsum + terms[0])

    key_start = (
        jnp.stack([keys, values]),
        jnp.zeros((2, tok_rows, heads_local, HD), jnp.float32),
        zero_rows,
    )
    key_final = lax.fori_loop(0, devices, key_turn, key_start)
    grad_queries = key_final[2]
    grad_keys = key_final[1][0]
    grad_values = key_final[1][1]
    grad_query_lin = (
        unrotate(grad_queries, cosine, sine)
        .reshape(tok_rows, heads_local * HD)
        .astype(jnp.bfloat16)
    )
    grad_key_lin = (
        unrotate(grad_keys, cosine, sine).reshape(tok_rows, heads_local * HD).astype(jnp.bfloat16)
    )
    grad_value_lin = grad_values.reshape(tok_rows, heads_local * HD).astype(jnp.bfloat16)
    grad_w_query = jnp.einsum(
        "td,tc->dc", hidden_attn, grad_query_lin, preferred_element_type=jnp.float32
    )
    grad_w_key = jnp.einsum(
        "td,tc->dc", hidden_attn, grad_key_lin, preferred_element_type=jnp.float32
    )
    grad_w_value = jnp.einsum(
        "td,tc->dc", hidden_attn, grad_value_lin, preferred_element_type=jnp.float32
    )
    attn_grad_part = jnp.einsum(
        "tc,dc->td", grad_query_lin, query_full, preferred_element_type=jnp.float32
    )
    attn_grad_part = attn_grad_part + jnp.einsum(
        "tc,dc->td", grad_key_lin, key_full, preferred_element_type=jnp.float32
    )
    attn_grad_part = attn_grad_part + jnp.einsum(
        "tc,dc->td", grad_value_lin, value_full, preferred_element_type=jnp.float32
    )
    grad_hidden_attn = lax.psum(attn_grad_part.astype(jnp.bfloat16), "tp").astype(jnp.float32)
    grad_gain_attn = jnp.sum(grad_hidden_attn * normed_attn, axis=0)
    grad_tokens = norm_back(grad_hidden_attn * gain_attn, normed_attn, inverse_attn) + grad_resid
    attn_shards = (
        lax.psum_scatter(grad_w_query, "seq", scatter_dimension=0, tiled=True),
        lax.psum_scatter(grad_w_key, "seq", scatter_dimension=0, tiled=True),
        lax.psum_scatter(grad_w_value, "seq", scatter_dimension=0, tiled=True),
        lax.psum_scatter(grad_w_out, "seq", scatter_dimension=1, tiled=True),
        lax.psum_scatter(grad_gain_attn, "seq", scatter_dimension=0, tiled=True),
    )
    return (
        output,
        grad_tokens,
        attn_shards[4],
        attn_shards[0],
        attn_shards[1],
        attn_shards[2],
        attn_shards[3],
        mlp_shards[3],
        mlp_shards[0],
        mlp_shards[1],
        mlp_shards[2],
    )


MESH = pl.DeviceIdType.MESH
ANY = pl.BlockSpec(memory_space=pl.ANY)
VMEM = pl.BlockSpec(memory_space=pltpu.VMEM)


def place():
    seq = lax.axis_index("seq")
    return (seq // 4, (seq // 2) % 2, seq % 2, lax.axis_index("tp"))


def device(z, y, x, core):
    return (z * 4 + y * 2 + x, core)


def meet(peers):
    barrier = pltpu.get_barrier_semaphore()
    for peer in peers:
        pl.semaphore_signal(barrier, inc=1, device_id=peer, device_id_type=MESH)
    pl.semaphore_wait(barrier, len(peers))


def push(source, target, send_sem, recv_sem, peer):
    copy = pltpu.make_async_remote_copy(
        src_ref=source,
        dst_ref=target,
        send_sem=send_sem,
        recv_sem=recv_sem,
        device_id=peer,
        device_id_type=MESH,
    )
    copy.start()
    return copy


def plane_peers():
    z, y, x, core = place()
    return [device((z + d) % 4, y, x, core) for d in (1, 2, 3)] + [
        device(z, 1 - y, x, core),
        device(z, y, x, 1 - core),
    ]


def gather_kernel(mine, out, send, recv, local):
    z, y, x, core = place()
    rows = mine.shape[0]
    meet(plane_peers())

    def slot(zz, yy, cc):
        return out.at[pl.ds(pl.multiple_of((zz * 4 + yy * 2 + cc) * rows, rows), rows)]

    keep = pltpu.make_async_copy(mine, slot(z, y, core), local)
    keep.start()
    sent = []

    def go(index, source, target, peer):
        copy = push(source, target, send.at[index], recv.at[index], peer)
        sent.append(copy)
        return copy

    along_z, along_y, across = {}, {}, {}
    for d in (1, 3, 2):
        along_z[d] = go(d - 1, mine, slot(z, y, core), device((z + d) % 4, y, x, core))
    along_y[0] = go(3, mine, slot(z, y, core), device(z, 1 - y, x, core))
    across[0] = go(7, mine, slot(z, y, core), device(z, y, x, 1 - core))
    for d in (1, 3, 2):
        along_z[d].wait_recv()
        part = slot((z - d) % 4, y, core)
        along_y[d] = go(3 + d, part, part, device(z, 1 - y, x, core))
        across[d] = go(7 + d, part, part, device(z, y, x, 1 - core))
    for d in (0, 1, 3, 2):
        along_y[d].wait_recv()
        part = slot((z - d) % 4, 1 - y, core)
        across[4 + d] = go(11 + d, part, part, device(z, y, x, 1 - core))
    for d in range(8):
        across[d].wait_recv()
    for copy in sent:
        copy.wait_send()
    keep.wait()


def gather_plane(mine):
    rows, width = mine.shape
    return pl.pallas_call(
        gather_kernel,
        out_shape=jax.ShapeDtypeStruct((rows * 16, width), mine.dtype),
        in_specs=[ANY],
        out_specs=ANY,
        scratch_shapes=[
            pltpu.SemaphoreType.DMA((15,)),
            pltpu.SemaphoreType.DMA((15,)),
            pltpu.SemaphoreType.DMA,
        ],
        compiler_params=pltpu.CompilerParams(collective_id=0, has_side_effects=True),
    )(mine)


def reduce_kernel(part, out, pair, half, ybuf, zsum, zbuf, send, recv):
    z, y, x, core = place()
    rows = out.shape[0]
    meet(plane_peers())

    def span(zz, yy, cc):
        return pl.ds(pl.multiple_of((zz * 4 + yy * 2 + cc) * rows, rows), rows)

    order = [(d, other) for other in (1, 0) for d in (2, 1, 3, 0)]
    across, along_y, along_z = {}, {}, {}
    for i, (d, other) in enumerate(order):
        zz, yy = (z + d) % 4, (y + other) % 2
        across[i] = push(
            part.at[span(zz, yy, 1 - core)],
            pair.at[i],
            send.at[i],
            recv.at[i],
            device(z, y, x, 1 - core),
        )
    f32 = jnp.float32
    for i, (d, other) in enumerate(order):
        zz, yy = (z + d) % 4, (y + other) % 2
        across[i].wait_recv()
        total = part[span(zz, yy, core)].astype(f32) + pair[i].astype(f32)
        half[i] = total.astype(half.dtype)
        if other:
            along_y[i] = push(
                half.at[i], ybuf.at[i], send.at[8 + i], recv.at[8 + i], device(z, 1 - y, x, core)
            )
    for i, (d, other) in enumerate(order[4:]):
        along_y[i].wait_recv()
        if d:
            total = half[4 + i].astype(f32) + ybuf[i].astype(f32)
            zsum[i] = total.astype(zsum.dtype)
            along_z[i] = push(
                zsum.at[i],
                zbuf.at[i],
                send.at[12 + i],
                recv.at[12 + i],
                device((z + d) % 4, y, x, core),
            )
    for i in range(3):
        along_z[i].wait_recv()
    out[...] = (half[7].astype(f32) + ybuf[3].astype(f32)) + (
        zbuf[0].astype(f32) + zbuf[1].astype(f32) + zbuf[2].astype(f32)
    )
    for copies in (across, along_y, along_z):
        for copy in copies.values():
            copy.wait_send()


def reduce_plane(part):
    rows, width = part.shape[0] // 16, part.shape[1]

    def room(count):
        return pltpu.VMEM((count, rows, width), part.dtype)

    return pl.pallas_call(
        reduce_kernel,
        out_shape=jax.ShapeDtypeStruct((rows, width), jnp.float32),
        in_specs=[VMEM],
        out_specs=VMEM,
        scratch_shapes=[
            room(8),
            room(8),
            room(4),
            room(3),
            room(3),
            pltpu.SemaphoreType.DMA((15,)),
            pltpu.SemaphoreType.DMA((15,)),
        ],
        compiler_params=pltpu.CompilerParams(collective_id=1, has_side_effects=True),
    )(part)


def weights_kernel(*refs):
    z, y, x, core = place()
    mine = z * 2 + y
    count = (len(refs) - 5) // 2
    groups, outs = refs[:count], refs[count : 2 * count]
    send, recv, xsend, xrecv, local = refs[2 * count :]
    mate = device(z, y, 1 - x, core)
    meet([device((z + d // 2) % 4, (y + d) % 2, x, core) for d in range(1, 8)] + [mate])

    def slot(group, zz, yy, xx):
        owner = (zz * 2 + yy) * 2 + xx
        out = outs[group]
        if group % 2 == 0:
            rows = groups[group].shape[1]
            return out.at[pl.ds(pl.multiple_of(owner * rows, rows), rows)]
        columns = groups[group].shape[2]
        return out.at[:, pl.ds(pl.multiple_of(owner * columns, columns), columns)]

    keeps, spread, passed = [], {}, []
    for group in range(count):
        keep = pltpu.make_async_copy(
            groups[group].at[mine], slot(group, z, y, x), local.at[group]
        )
        keep.start()
        keeps.append(keep)
        passed.append(
            push(
                groups[group].at[mine],
                slot(group, z, y, x),
                xsend.at[group, 0],
                xrecv.at[group, 0],
                mate,
            )
        )
        for d in (4, 5, 2, 3, 6, 7, 1):
            zz, yy = (z + d // 2) % 4, (y + d) % 2
            spread[group, d] = push(
                groups[group].at[zz * 2 + yy],
                slot(group, z, y, x),
                send.at[group, d],
                recv.at[group, d],
                device(zz, yy, x, core),
            )
    for group in range(count):
        for d in (1, 2, 3, 6, 7, 4, 5):
            spread[group, d].wait_recv()
            part = slot(group, (z - d // 2) % 4, (y + d) % 2, x)
            passed.append(push(part, part, xsend.at[group, d], xrecv.at[group, d], mate))
    for copy in passed:
        copy.wait_recv()
    for copy in passed:
        copy.wait_send()
    for copy in spread.values():
        copy.wait_send()
    for keep in keeps:
        keep.wait()


def spread_weights(groups):
    shapes = []
    for index, group in enumerate(groups):
        _, rows, columns = group.shape
        whole = (rows * 16, columns) if index % 2 == 0 else (rows, columns * 16)
        shapes.append(jax.ShapeDtypeStruct(whole, group.dtype))
    count = len(groups)
    return pl.pallas_call(
        weights_kernel,
        out_shape=shapes,
        in_specs=[ANY] * count,
        out_specs=[ANY] * count,
        scratch_shapes=[pltpu.SemaphoreType.DMA((count, 8))] * 4
        + [pltpu.SemaphoreType.DMA((count,))],
        compiler_params=pltpu.CompilerParams(collective_id=2, has_side_effects=True),
    )(*groups)


def swap_kernel(mine, other, send, recv, *, across):
    z, y, x, core = place()
    peer = device(z, y, x, 1 - core) if across else device(z, y, 1 - x, core)
    meet([peer])
    push(mine, other, send, recv, peer).wait()


def swap(mine, across, ident):
    return pl.pallas_call(
        functools.partial(swap_kernel, across=across),
        out_shape=jax.ShapeDtypeStruct(mine.shape, mine.dtype),
        in_specs=[ANY],
        out_specs=ANY,
        scratch_shapes=[pltpu.SemaphoreType.DMA] * 2,
        compiler_params=pltpu.CompilerParams(
            collective_id=ident, has_side_effects=True
        ),
    )(mine)


def return_kernel(*refs):
    z, y, x, core = place()
    mine = z * 2 + y
    count = (len(refs) - 3) // 2
    groups, outs = refs[:count], refs[count : 2 * count]
    send, recv, local = refs[2 * count :]
    meet([device((z + d // 2) % 4, (y + d) % 2, x, core) for d in range(1, 8)])
    copies, keeps = [], []
    for group in range(count):
        keep = pltpu.make_async_copy(
            groups[group].at[mine], outs[group].at[mine], local.at[group]
        )
        keep.start()
        keeps.append(keep)
        for d in (4, 5, 2, 3, 6, 7, 1):
            zz, yy = (z + d // 2) % 4, (y + d) % 2
            copies.append(
                push(
                    groups[group].at[zz * 2 + yy],
                    outs[group].at[mine],
                    send.at[group, d],
                    recv.at[group, d],
                    device(zz, yy, x, core),
                )
            )
    for copy in copies:
        copy.wait_recv()
    for copy in copies:
        copy.wait_send()
    for keep in keeps:
        keep.wait()


def return_grads(groups):
    count = len(groups)
    return pl.pallas_call(
        return_kernel,
        out_shape=[jax.ShapeDtypeStruct(group.shape, group.dtype) for group in groups],
        in_specs=[ANY] * count,
        out_specs=[ANY] * count,
        scratch_shapes=[pltpu.SemaphoreType.DMA((count, 8))] * 2
        + [pltpu.SemaphoreType.DMA((count,))],
        compiler_params=pltpu.CompilerParams(collective_id=5, has_side_effects=True),
    )(*groups)


def plane_positions(block_order, x, tok_rows, group_rows):
    rows = jnp.arange(tok_rows * 8, dtype=jnp.int32)
    stored = (rows // tok_rows) * (2 * tok_rows) + x * tok_rows + rows % tok_rows
    slots = jnp.arange(block_order.shape[0], dtype=jnp.int32)
    onehot = ((stored // group_rows)[:, None] == slots[None, :]).astype(jnp.int32)
    return jnp.sum(onehot * block_order[None, :], axis=1) * group_rows + stored % group_rows


def turn(values, cosine, sine):
    half_dim = values.shape[-1] // 2
    first, second = values[..., :half_dim], values[..., half_dim:]
    return jnp.concatenate(
        [first * cosine - second * sine, second * cosine + first * sine], axis=-1
    )


def per_device_split(
    tokens,
    cotangent,
    block_order,
    sequence_ids,
    attn_gain,
    w_query,
    w_key,
    w_value,
    w_out,
    mlp_gain,
    w_gate,
    w_up,
    w_down,
):
    bf16, f32 = jnp.bfloat16, jnp.float32
    tok_rows, width = tokens.shape
    own = tok_rows // 2
    score_bias = -math.log(tok_rows * 16 // 2)
    score_scale = 1.0 / math.sqrt(HD)
    z, y, x, core = place()
    boundary = jnp.sum((sequence_ids == 0).astype(jnp.int32))
    my_pos = plane_positions(block_order, x, tok_rows, own)
    key_pos = jnp.concatenate([my_pos, plane_positions(block_order, 1 - x, tok_rows, own)])
    my_start = jnp.where(my_pos >= boundary, boundary, 0)
    allowed = (key_pos[None, :] <= my_pos[:, None]) & (key_pos[None, :] >= my_start[:, None])

    def by_columns(weight):
        rows, columns = weight.shape
        return weight.astype(bf16).reshape(rows, 8, columns // 8).transpose(1, 0, 2)

    def by_rows(weight):
        rows, columns = weight.shape
        return weight.astype(bf16).reshape(8, rows // 8, columns)

    groups = (
        jnp.concatenate([by_columns(w_query), by_columns(w_key), by_columns(w_value)], axis=2),
        by_rows(w_out),
        jnp.concatenate([by_columns(w_gate), by_columns(w_up)], axis=2),
        by_rows(w_down),
    )
    head_in, head_out, hidden_in, hidden_out = spread_weights(groups)
    gains = lax.all_gather(jnp.stack([attn_gain, mlp_gain]), "seq", axis=1, tiled=True)
    gains = gains.astype(bf16).astype(f32)
    gain_attn, gain_mlp = gains[0], gains[1]
    tokens_own = lax.dynamic_slice_in_dim(tokens, core * own, own, 0)
    cot_own = lax.dynamic_slice_in_dim(cotangent, core * own, own, 0)
    source = gather_plane(tokens_own).astype(f32)
    cot = gather_plane(cot_own)
    normed_attn, _ = normalize(source)
    hidden_attn = (normed_attn * gain_attn).astype(bf16)
    cosine, sine = rope_tables(my_pos, HD)
    qkv = jnp.dot(hidden_attn, head_in, preferred_element_type=f32)
    query = turn(qkv[:, :HD], cosine, sine).astype(bf16)
    key = turn(qkv[:, HD : 2 * HD], cosine, sine).astype(bf16)
    key_value = jnp.concatenate([key, qkv[:, 2 * HD :].astype(bf16)], axis=1)
    key_value = jnp.concatenate([key_value, swap(key_value, False, 3)], axis=0)
    keys, values = key_value[:, :HD], key_value[:, HD:]
    scores = jnp.dot(query, keys.T, preferred_element_type=f32) * score_scale + score_bias
    sigmas = jax.nn.sigmoid(scores)
    weights = jnp.where(allowed, sigmas, 0.0).astype(bf16)
    attended = jnp.dot(weights, values, preferred_element_type=f32).astype(bf16)
    attn_part = jnp.dot(attended, head_out, preferred_element_type=f32).astype(bf16)
    residual = tokens_own.astype(f32) + reduce_plane(attn_part)
    normed_mlp, inverse_mlp = normalize(residual)
    hidden_mlp = gather_plane((normed_mlp * gain_mlp).astype(bf16))
    gate_up = jnp.dot(hidden_mlp, hidden_in, preferred_element_type=f32)
    units = gate_up.shape[1] // 2
    gate, up_proj = gate_up[:, :units], gate_up[:, units:]
    gate_sigma = jax.nn.sigmoid(gate)
    gate_silu = gate * gate_sigma
    activated = (gate_silu * up_proj).astype(bf16)
    grad_act = jnp.dot(cot, hidden_out.T, preferred_element_type=f32)
    grad_gate_act = (grad_act * up_proj * gate_sigma * (1.0 + gate * (1.0 - gate_sigma))).astype(
        bf16
    )
    grad_pair = jnp.concatenate([grad_gate_act, (grad_act * gate_silu).astype(bf16)], axis=1)
    hidden_grad_part = jnp.dot(grad_pair, hidden_in.T, preferred_element_type=f32).astype(bf16)
    grad_hidden_mlp = reduce_plane(hidden_grad_part)
    mlp_part = jnp.dot(activated, hidden_out, preferred_element_type=f32).astype(bf16)
    output_own = (residual + reduce_plane(mlp_part)).astype(bf16)
    grad_gain_mlp = jnp.sum(grad_hidden_mlp * normed_mlp, axis=0)
    grad_resid = norm_back(grad_hidden_mlp * gain_mlp, normed_mlp, inverse_mlp) + cot_own.astype(
        f32
    )
    resid_low = gather_plane(grad_resid.astype(bf16))
    grad_head_out = jnp.dot(attended.T, resid_low, preferred_element_type=f32)
    grad_attended = jnp.dot(resid_low, head_out.T, preferred_element_type=f32).astype(bf16)
    grad_values = jnp.dot(weights.T, grad_attended, preferred_element_type=f32)
    grad_weights = jnp.dot(grad_attended, values.T, preferred_element_type=f32)
    grad_scores = jnp.where(allowed, grad_weights * sigmas * (1.0 - sigmas), 0.0).astype(bf16)
    grad_query = jnp.dot(grad_scores, keys, preferred_element_type=f32) * score_scale
    grad_keys = jnp.dot(grad_scores.T, query, preferred_element_type=f32) * score_scale
    grad_kv = jnp.concatenate([grad_keys, grad_values], axis=1)
    plane_rows = tok_rows * 8
    grad_kv = grad_kv[:plane_rows] + swap(grad_kv[plane_rows:].astype(bf16), False, 3).astype(f32)
    grad_lin = jnp.concatenate(
        [
            turn(grad_query, cosine, -sine).astype(bf16),
            turn(grad_kv[:, :HD], cosine, -sine).astype(bf16),
            grad_kv[:, HD:].astype(bf16),
        ],
        axis=1,
    )
    attn_grad_part = jnp.dot(grad_lin, head_in.T, preferred_element_type=f32).astype(bf16)
    grad_hidden_attn = reduce_plane(attn_grad_part)
    normed_own, inverse_own = normalize(tokens_own.astype(f32))
    grad_gain_attn = jnp.sum(grad_hidden_attn * normed_own, axis=0)
    grad_tokens_own = norm_back(grad_hidden_attn * gain_attn, normed_own, inverse_own) + grad_resid

    def whole_rows(mine, ident):
        other = swap(mine, True, ident)
        first = jnp.where(core == 0, mine, other)
        second = jnp.where(core == 0, other, mine)
        return jnp.concatenate([first, second], axis=0)

    grad_head_in = jnp.dot(hidden_attn.T, grad_lin, preferred_element_type=f32)
    grad_hidden_in = jnp.dot(hidden_mlp.T, grad_pair, preferred_element_type=f32)
    grad_hidden_out = jnp.dot(activated.T, cot, preferred_element_type=f32)

    def rows_of(grad):
        return grad.reshape(8, 2, grad.shape[0] // 16, grad.shape[1]).transpose(1, 0, 2, 3)

    def columns_of(grad):
        split = grad.reshape(grad.shape[0], 8, 2, grad.shape[1] // 16)
        return split.transpose(2, 1, 0, 3)

    def joined(split, ident):
        mine = lax.dynamic_index_in_dim(split, x, 0, keepdims=False)
        other = lax.dynamic_index_in_dim(split, 1 - x, 0, keepdims=False).astype(bf16)
        return (mine + swap(other, False, ident).astype(f32)).astype(bf16)

    returned = return_grads(
        (
            joined(jnp.concatenate([rows_of(grad_head_in), rows_of(grad_hidden_in)], axis=3), 8),
            joined(
                jnp.concatenate([columns_of(grad_head_out), columns_of(grad_hidden_out)], axis=2), 9
            ),
        )
    )
    into, outof = returned[0].astype(f32), returned[1].astype(f32)

    def columns_back(first, count):
        piece = into[:, :, first : first + count].transpose(1, 0, 2)
        return piece.reshape(piece.shape[0], 8 * count)

    def rows_back(first, count):
        return outof[:, first : first + count].reshape(8 * count, outof.shape[2])

    gain_sums = lax.psum(jnp.stack([grad_gain_attn, grad_gain_mlp]), ("seq", "tp"))
    mine = lax.dynamic_slice_in_dim(gain_sums, lax.axis_index("seq") * tok_rows, tok_rows, 1)
    return (
        whole_rows(output_own, 6),
        whole_rows(grad_tokens_own, 7),
        mine[0],
        columns_back(0, HD),
        columns_back(HD, HD),
        columns_back(2 * HD, HD),
        rows_back(0, HD),
        mine[1],
        columns_back(3 * HD, units),
        columns_back(3 * HD + units, units),
        rows_back(HD, units),
    )


def solution(mesh):
    in_specs = (
        P("seq", None),
        P("seq", None),
        P(),
        P(),
        P("seq"),
        P("seq", "tp"),
        P("seq", "tp"),
        P("seq", "tp"),
        P("tp", "seq"),
        P("seq"),
        P("seq", "tp"),
        P("seq", "tp"),
        P("tp", "seq"),
    )
    out_specs = (
        P("seq", None),
        P("seq", None),
        P("seq"),
        P("seq", "tp"),
        P("seq", "tp"),
        P("seq", "tp"),
        P("tp", "seq"),
        P("seq"),
        P("seq", "tp"),
        P("seq", "tp"),
        P("tp", "seq"),
    )
    fits = mesh.shape["seq"] == 16 and mesh.shape["tp"] == 2
    return jax.shard_map(
        per_device_split if fits else per_device_gathered, mesh=mesh, in_specs=in_specs, out_specs=out_specs, check_vma=False
    )
```
